1024 devices in a mesh: dp: 32 (over y, z_lo), expert: 32 (over x, z_hi, core).
Axes of the slice: x: 8, y: 8, z: 8 (z_hi: 2, z_lo: 4; z = z_hi * 4 + z_lo), core: 2. Of those that a mesh axis runs over, the one named last changes fastest.
Arguments:
- tokens: bfloat16 [131072, 3584], P(('dp', 'expert')), may hold values from -6 to 6
- routes: int32 [131072, 1], P(('dp', 'expert')), may hold values from 0 to 31; in each aligned block of 128 rows (0 to 127, 128 to 255, ...) at most 6 rows name the same one
- gates: float32 [131072, 1], P(('dp', 'expert')), may hold values from 0.1 to 1
- counts: int32 [1024], P(('dp', 'expert')), may hold values from 16 to 128, as said below
- expert_weight: bfloat16 [32, 3584, 1024], P('expert'), may hold values from -0.09375 to 0.09375
- cotangent: bfloat16 [131072, 1024], P(('dp', 'expert')), may hold values from -6 to 6
Outputs:
- mixed: bfloat16 [131072, 1024], P(('dp', 'expert'))
- token_grad: bfloat16 [131072, 3584], P(('dp', 'expert'))
- gate_grad: float32 [131072, 1], P(('dp', 'expert'))
The draws below stay inside these ranges and needn't reach their ends.
Inputs may be any that keep to these rules, and one draw needn't show every extreme that they name: `routes`: among the tokens of one device at most 6 name one expert; some device sends exactly 6 to some expert; every expert is named. The first counts[i] tokens of device i are valid; some device has all of its tokens valid.
All inputs are finite; a program needn't handle non-finite values.
Results may differ from the reference program's by a relative error of at most 0.0058.
Values may be sent and summed in bfloat16 or wider, within the bound.
No kernel may reach another device: no remote copies, remote signals or barrier semaphores. Data moves between devices by JAX's collectives and lax.ppermute only.
A program may use at most 32 MiB of HBM per device.

```python
import math
import jax
import jax.numpy as jnp
import numpy as np
from jax import lax

D = 3584
H = 1024
TOK_DEV = 128
EXPERTS = 32
CAP = 6
TOKENS = 131072
N_EXPERT = 32
DEVICES = 1024


def draw_counts(key, part):
    number = DEVICES
    level = jax.random.randint(jax.random.fold_in(key, 11), (), TOK_DEV // 8, TOK_DEV // 4 + 1)
    upward = jax.random.randint(jax.random.fold_in(key, 12), (), 0, 2)
    index = jnp.arange(number, dtype=jnp.int32)
    place = jnp.where(upward == 1, index, number - 1 - index).astype(jnp.int32)
    ramp = level + 2 * level * place // max(number - 1, 1)
    noise = jax.random.randint(jax.random.fold_in(key, 13), (number,), 0, 1048576)
    jitter = noise % (ramp + 1)
    values = jnp.minimum(TOK_DEV, ramp + jitter)
    full_one = jax.random.randint(jax.random.fold_in(key, 14), (), 0, number)
    offset = jax.random.randint(jax.random.fold_in(key, 15), (), 0, number - 1)
    low_one = (full_one + 1 + offset) % number
    values = jnp.where(index == full_one, TOK_DEV, values)
    values = jnp.where(index == low_one, TOK_DEV // 8, values)
    return values.astype(jnp.int32)


def levels(key, shape, pieces, least, top_value):
    def one(dim, blocks):
        heights = jax.random.uniform(jax.random.fold_in(jax.random.fold_in(key, 6), dim), (blocks,), jnp.float32, least / len(pieces), top_value / len(pieces))
        return jnp.repeat(jnp.exp(heights), shape[dim] // blocks).reshape((-1,) + (1,) * (len(shape) - dim - 1))

    level = one(*pieces[0])
    for cut in pieces[1:]:
        level = level * one(*cut)
    return level


def shared_out(rng, own, number, rows, amount, top, most, lean):
    order = jax.random.permutation(rng, amount)
    heavy_load, common = shares(amount, rows * top, most, lean, True), shares(amount, rows * top, most, lean, False)
    places = jnp.arange(amount)

    def named(lengths, offset_by):
        used = int((lengths > 0).sum())
        fixed = max(1, used // 4)
        moved = fixed + (places - fixed + offset_by * (used - fixed)) % max(1, amount - fixed)
        return jnp.zeros((amount,), jnp.int32).at[order[jnp.where(places < fixed, places, moved)]].set(jnp.asarray(lengths, jnp.int32))

    lengths = jnp.where(number % 4 == 0, named(heavy_load, number // 4), named(common, number - number // 4 - 1))
    mixed = jax.random.permutation(jax.random.fold_in(own, 3), amount)
    source_of, sink = mixed[0:amount // 2 * 2:2], mixed[1:amount // 2 * 2:2]
    margin = jnp.minimum(lengths[source_of] - 1, most - lengths[sink]) // 2
    margin = jnp.where((source_of == order[0]) | (sink == order[0]) | (lengths[sink] == 0), 0, jnp.maximum(margin, 0))
    moved = jax.random.randint(jax.random.fold_in(own, 4), (amount // 2,), 0, 1 << 20) % (margin + 1)
    lengths = lengths.at[source_of].add(-moved).at[sink].add(moved)
    labels = jnp.searchsorted(jnp.cumsum(lengths), jnp.arange(rows * top), side="right").astype(jnp.int32)
    grid = labels.reshape(top, rows).T
    grid = grid[jax.random.permutation(jax.random.fold_in(own, 1), rows)]
    offset_by = jax.random.randint(jax.random.fold_in(own, 2), (rows, 1), 0, top)
    return jnp.take_along_axis(grid, (jnp.arange(top)[None, :] + offset_by) % top, axis=1)


def shares(amount, total, reach, skew, full):
    weights = [(1 << 20) // math.isqrt(rank ** skew) + 1 for rank in range(1, amount + 1)]
    largest = reach if full else min(reach, max(-(-total // amount), total * weights[0] // sum(weights)))
    least = 1 if total - largest >= amount - 1 else 0
    given, rest = [largest] + [least] * (amount - 1), total - largest - least * (amount - 1)
    while rest > 0:
        free = [i for i in range(1, amount) if given[i] < largest] or [i for i in range(1, amount) if given[i] < reach]
        pool, budget = sum([weights[i] for i in free]), rest
        for i in free:
            more = min(reach - given[i], max(1, budget * weights[i] // pool), rest)
            given[i] = given[i] + more
            rest = rest - more
    return np.array(given)


def centred(stream_key, extent, width, bound, pieces=(), kind=jnp.bfloat16):
    result = jax.random.normal(stream_key, extent, jnp.float32) * width
    if len(pieces) > 0:
        result = levels(stream_key, extent, pieces, -0.22, 0.18) * result
    return jnp.clip(result, min=-bound, max=bound).astype(kind)


def setup_inputs(seed: int = 0) -> dict:
    arg_keys = jax.random.split(jax.random.key(seed), 7)
    tokens = centred(arg_keys[0], (TOKENS, D), 1.0, 6.0, ((0, 1024),))
    routes_keys = jax.random.split(jax.random.fold_in(arg_keys[1], 1), TOKENS // TOK_DEV)
    routes_turns = jax.random.permutation(jax.random.fold_in(arg_keys[1], 3), TOKENS // TOK_DEV)
    routes = jax.vmap(lambda own, number: shared_out(jax.random.fold_in(arg_keys[1], 2), own, number, TOK_DEV, N_EXPERT, 1, CAP, 2))(routes_keys, routes_turns).reshape((TOKENS, 1))
    gates = jnp.clip(jnp.exp(math.log(1.0) - 2.3025851 * jax.random.uniform(arg_keys[2], (TOKENS, 1), jnp.float32) ** levels(arg_keys[2], (TOKENS, 1), ((0, 1024),), -0.2, 0.2)), 0.1, 1.0)
    counts = draw_counts(jax.random.fold_in(arg_keys[6], 71), 0)
    expert_weight = centred(arg_keys[4], (EXPERTS, D, H), D ** -0.5, 0.09375, ((0, 32),))
    cotangent = centred(arg_keys[5], (TOKENS, H), 1.0, 6.0, ((0, 1024),))
    return dict(tokens=tokens, routes=routes, gates=gates, counts=counts, expert_weight=expert_weight, cotangent=cotangent)


def reference(tokens, routes, gates, counts, expert_weight, cotangent):
    total_rows = tokens.shape[0]
    route = routes[:, 0]
    gate = gates[:, 0]
    position = jnp.arange(total_rows, dtype=jnp.int32)
    owner = (position // TOK_DEV).astype(jnp.int32)
    valid = ((position % TOK_DEV) < counts[owner]).astype(jnp.float32)
    total = jnp.sum(counts.astype(jnp.float32))
    scale = jnp.float32(total_rows) / total
    factor = valid * scale
    upstream = ((gate * factor)[:, None] * cotangent.astype(jnp.float32)).astype(jnp.bfloat16)
    order = jnp.argsort(route, stable=True).astype(jnp.int32)
    loads = jnp.bincount(route, length=EXPERTS).astype(jnp.int32)
    starts = (jnp.cumsum(loads) - loads).astype(jnp.int32)
    span = DEVICES * CAP
    padded_order = jnp.concatenate([order, jnp.zeros((span,), jnp.int32)])

    def step(carry, expert):
        act_all, grad_all = carry
        index = lax.dynamic_slice_in_dim(padded_order, starts[expert], span)
        live = jnp.arange(span, dtype=jnp.int32) < loads[expert]
        target = jnp.where(live, index, total_rows).astype(jnp.int32)
        weight = expert_weight[expert]
        pre = jnp.dot(tokens[index], weight, preferred_element_type=jnp.float32)
        sig = jax.nn.sigmoid(pre)
        act = (pre * sig).astype(jnp.bfloat16)
        slope = sig * (1.0 + pre * (1.0 - sig))
        delta = (upstream[index].astype(jnp.float32) * slope).astype(jnp.bfloat16)
        back = jnp.dot(delta, weight.T, preferred_element_type=jnp.float32).astype(jnp.bfloat16)
        act_all = act_all.at[target].set(act, mode="drop")
        grad_all = grad_all.at[target].set(back, mode="drop")
        return (act_all, grad_all), None

    start = (jnp.zeros((total_rows, H), jnp.bfloat16), jnp.zeros((total_rows, D), jnp.bfloat16))
    (act_all, grad_all), _ = lax.scan(step, start, jnp.arange(EXPERTS, dtype=jnp.int32))
    act_float = act_all.astype(jnp.float32)
    mixed = (gate[:, None] * act_float).astype(jnp.bfloat16)
    gate_grad = (jnp.sum(act_float * cotangent.astype(jnp.float32), axis=1) * factor)[:, None]
    return mixed, grad_all, gate_grad
```

```python
import functools

import jax
import jax.numpy as jnp
from jax import lax
from jax.experimental import pallas as pl
from jax.experimental.pallas import tpu as pltpu
from jax.sharding import Mesh, PartitionSpec as P

ROWS = 8
SLOTS = 6
PARTS = 3

BF = jnp.bfloat16
F32 = jnp.float32


def dot(a, b, dims=(((1,), (0,)), ((), ()))):
    return lax.dot_general(a, b, dims, preferred_element_type=F32)


def iota(shape, axis):
    return lax.broadcasted_iota(jnp.int32, shape, axis)


def places(route, experts):
    tokens = route.shape[1]
    choose = (iota((experts, tokens), 0) == route).astype(F32)
    before = (iota((tokens, tokens), 0) < iota((tokens, tokens), 1)).astype(BF)
    rank = jnp.sum(dot(choose.astype(BF), before) * choose, axis=0, keepdims=True).astype(jnp.int32)
    late = (rank >= PARTS).astype(jnp.int32)
    part = rank - PARTS * late
    row = iota((experts * ROWS, tokens), 0)
    main = row == route * ROWS + rank
    tail = row == route * ROWS + (SLOTS + late)
    return main, [jnp.logical_and(tail, part == i) for i in range(PARTS)]


def column(row):
    n = row.shape[1]
    return jnp.sum(jnp.where(iota((n, n), 0) == iota((n, n), 1), row, 0.0), axis=1, keepdims=True)


def line(col):
    n = col.shape[0]
    return jnp.sum(jnp.where(iota((n, n), 0) == iota((n, n), 1), col, 0.0), axis=0, keepdims=True)


def slot_part(rows, part, axis):
    slot, tail = iota((rows, rows), axis), iota((rows, rows), 1 - axis)
    inner = jnp.bitwise_and(tail, ROWS - 1)
    want = tail - inner + PARTS * (inner - SLOTS) + part
    return jnp.logical_and(inner >= SLOTS, slot == want).astype(BF)


def pack_kernel(count, route, gate, tokens, cotangent, out):
    experts = out.shape[0] // ROWS
    main, tails = places(route[...], experts)
    local = route.shape[1]
    weight = jnp.where(iota((1, local), 1) < count[0], gate[...], 0.0)
    main = main.astype(BF)
    width = out.shape[1] // PARTS
    wide = out.shape[1]
    for i in range(PARTS):
        place = tails[i].astype(BF)
        factor = jnp.sum(jnp.where(tails[i], weight, 0.0), axis=1, keepdims=True)
        rest = jnp.concatenate(
            [dot(place, tokens[:, wide:]), dot(place, cotangent[...]) * factor], axis=1
        )
        body = dot(main, tokens[:, i * width : (i + 1) * width])
        out[:, i * width : (i + 1) * width] = (body + rest).astype(BF)


def expert_kernel(scale, data, weight, out):
    rows, wide = data.shape
    width = wide // PARTS
    tail = weight.shape[0] - wide
    rest = dot(slot_part(rows, 0, 0), data[:, :width])
    for i in range(1, PARTS):
        rest = rest + dot(slot_part(rows, i, 0), data[:, i * width : (i + 1) * width])
    pre = dot(data[...], weight[:wide, :]) + dot(rest[:, :tail].astype(BF), weight[wide:, :])
    sig = 1.0 / (1.0 + jnp.exp(-pre))
    act = (pre * sig).astype(BF)
    slope = sig * (1.0 + pre * (1.0 - sig))
    delta = (rest[:, tail:] * slope).astype(BF)
    turned = (((1,), (1,)), ((), ()))
    last = (dot(delta, weight[wide:, :], turned) * scale[0]).astype(BF)
    home = jnp.concatenate([last, act], axis=1)
    for i in range(PARTS):
        cols = slice(i * width, (i + 1) * width)
        grad = dot(delta, weight[cols, :], turned) * scale[0]
        out[:, cols] = (grad + dot(slot_part(rows, i, 1), home)).astype(BF)


def unpack_kernel(count, scale, route, gate, data, cotangent, mixed, token_grad, gate_grad):
    experts = data.shape[0] // ROWS
    main, tails = places(route[...], experts)
    local = route.shape[1]
    wide = data.shape[1]
    width = wide // PARTS
    turned = (((0,), (0,)), ((), ()))
    main = main.astype(BF)
    rest = None
    for i in range(PARTS):
        cols = slice(i * width, (i + 1) * width)
        token_grad[:, cols] = dot(main, data[:, cols], turned).astype(BF)
        more = dot(tails[i].astype(BF), data[:, cols], turned)
        rest = more if rest is None else rest + more
    tail = token_grad.shape[1] - wide
    token_grad[:, wide:] = rest[:, :tail].astype(BF)
    act = rest[:, tail:]
    mixed[...] = (column(gate[...]) * act).astype(BF)
    total = jnp.sum(act * cotangent[...].astype(F32), axis=1, keepdims=True)
    factor = jnp.where(iota((1, local), 1) < count[0], scale[0], 0.0)
    gate_grad[...] = line(total) * factor


VM = pl.BlockSpec(memory_space=pltpu.VMEM)
SM = pl.BlockSpec(memory_space=pltpu.SMEM)


def call(kernel, ins, outs, name, flops):
    return pl.pallas_call(
        kernel,
        in_specs=ins,
        out_specs=[VM] * len(outs) if isinstance(outs, list) else VM,
        out_shape=outs,
        name=name,
        cost_estimate=pl.CostEstimate(flops=flops, bytes_accessed=10_000_000, transcendentals=0),
        compiler_params=pltpu.CompilerParams(vmem_limit_bytes=48 << 20),
    )


def shards(tokens, routes, gates, counts, expert_weight, cotangent):
    local, deep = tokens.shape
    units = cotangent.shape[1]
    experts = lax.axis_size("x") * lax.axis_size("zh") * lax.axis_size("core")
    devices = experts * lax.axis_size("y") * lax.axis_size("zl")
    group = ("x", "zh", "core")
    rows = experts * ROWS
    wide = (deep + units) * SLOTS // ROWS
    route = routes.reshape(1, local)
    gate = gates.reshape(1, local)
    weight = expert_weight[0]
    payload = call(
        pack_kernel,
        [SM, VM, VM, VM, VM],
        jax.ShapeDtypeStruct((rows, wide), BF),
        "pack",
        2 * rows * local * 2 * wide,
    )(counts, route, gate, tokens, cotangent)
    arrived = lax.all_to_all(
        payload.reshape(experts, ROWS, wide), group, split_axis=0, concat_axis=0, tiled=True
    )
    total = counts.astype(F32)
    for axis in ("y", ("zh", "zl"), "x", "core"):
        total = lax.psum(total, axis)
    scale = jnp.float32(local * devices) / total
    back = call(
        expert_kernel,
        [SM, VM, VM],
        jax.ShapeDtypeStruct((rows, wide), BF),
        "expert",
        4 * rows * deep * units,
    )(scale, arrived.reshape(rows, wide), weight)
    home = lax.all_to_all(
        back.reshape(experts, ROWS, wide), group, split_axis=0, concat_axis=0, tiled=True
    )
    mixed, token_grad, gate_grad = call(
        unpack_kernel,
        [SM, SM, VM, VM, VM, VM],
        [
            jax.ShapeDtypeStruct((local, units), BF),
            jax.ShapeDtypeStruct((local, deep), BF),
            jax.ShapeDtypeStruct((1, local), F32),
        ],
        "unpack",
        2 * rows * local * 2 * wide,
    )(counts, scale, route, gate, home.reshape(rows, wide), cotangent)
    return (mixed, token_grad, gate_grad.reshape(local, 1))


def solution(mesh):
    fine = Mesh(mesh.devices.reshape(8, 4, 8, 2, 2), ("y", "zl", "x", "zh", "core"))
    every = ("y", "zl", "x", "zh", "core")
    placed = (
        P(every, None),
        P(every, None),
        P(every, None),
        P(every),
        P(("x", "zh", "core"), None, None),
        P(every, None),
    )
    return jax.shard_map(
        shards,
        mesh=fine,
        in_specs=placed,
        out_specs=(P(every, None), P(every, None), P(every, None)),
        check_vma=False,
    )
```

```python
import functools

import jax
import jax.numpy as jnp
from jax import lax
from jax.experimental import pallas as pl
from jax.experimental.pallas import tpu as pltpu
from jax.sharding import Mesh, PartitionSpec as P

ROWS = 8
SLOTS = 6
PARTS = 3

BF = jnp.bfloat16
F32 = jnp.float32


def dot(a, b, dims=(((1,), (0,)), ((), ()))):
    return lax.dot_general(a, b, dims, preferred_element_type=F32)


def iota(shape, axis):
    return lax.broadcasted_iota(jnp.int32, shape, axis)


def places(route, experts):
    tokens = route.shape[1]
    choose = (iota((experts, tokens), 0) == route).astype(F32)
    before = (iota((tokens, tokens), 0) < iota((tokens, tokens), 1)).astype(BF)
    rank = jnp.sum(dot(choose.astype(BF), before) * choose, axis=0, keepdims=True).astype(jnp.int32)
    late = (rank >= PARTS).astype(jnp.int32)
    part = rank - PARTS * late
    row = iota((experts * ROWS, tokens), 0)
    main = row == route * ROWS + rank
    tail = row == route * ROWS + (SLOTS + late)
    return main, [jnp.logical_and(tail, part == i) for i in range(PARTS)]


def column(row):
    n = row.shape[1]
    return jnp.sum(jnp.where(iota((n, n), 0) == iota((n, n), 1), row, 0.0), axis=1, keepdims=True)


def line(col):
    n = col.shape[0]
    return jnp.sum(jnp.where(iota((n, n), 0) == iota((n, n), 1), col, 0.0), axis=0, keepdims=True)


def slot_part(rows, part, axis):
    slot, tail = iota((rows, rows), axis), iota((rows, rows), 1 - axis)
    inner = jnp.bitwise_and(tail, ROWS - 1)
    want = tail - inner + PARTS * (inner - SLOTS) + part
    return jnp.logical_and(inner >= SLOTS, slot == want).astype(BF)


def pack_kernel(count, route_in, gate_in, tokens_in, cotangent_in, out_hbm, route, gate, tokens, cotangent, out, sems):
    local, deep = tokens.shape
    wide = out.shape[1]
    width = wide // PARTS
    edges = [i * width for i in range(PARTS)] + [wide, deep]

    def piece(i):
        cols = pl.ds(edges[i], edges[i + 1] - edges[i])
        return pltpu.make_async_copy(tokens_in.at[:, cols], tokens.at[:, cols], sems.at[i])

    small = [
        pltpu.make_async_copy(route_in, route, sems.at[PARTS + 1]),
        pltpu.make_async_copy(gate_in, gate, sems.at[PARTS + 2]),
    ]
    side = pltpu.make_async_copy(cotangent_in, cotangent, sems.at[PARTS + 3])
    pieces = [piece(i) for i in range(PARTS + 1)]
    for copy in small + [pieces[PARTS], side] + pieces[:PARTS]:
        copy.start()
    for copy in small:
        copy.wait()
    main, tails = places(route[...], out.shape[0] // ROWS)
    weight = jnp.where(iota((1, local), 1) < count[0], gate[...], 0.0)
    main = main.astype(BF)
    factors = [
        jnp.sum(jnp.where(tail, weight, 0.0), axis=1, keepdims=True) for tail in tails
    ]
    pieces[PARTS].wait()
    side.wait()
    sent = []
    for i in range(PARTS):
        cols = slice(i * width, (i + 1) * width)
        place = tails[i].astype(BF)
        rest = jnp.concatenate(
            [dot(place, tokens[:, wide:]), dot(place, cotangent[...]) * factors[i]], axis=1
        )
        pieces[i].wait()
        out[:, cols] = (dot(main, tokens[:, cols]) + rest).astype(BF)
        copy = pltpu.make_async_copy(
            out.at[:, pl.ds(i * width, width)],
            out_hbm.at[:, pl.ds(i * width, width)],
            sems.at[PARTS + 4 + i],
        )
        copy.start()
        sent.append(copy)
    for copy in sent:
        copy.wait()


def expert_kernel(total, data, weight_in, out, total_out, weight, sems):
    total_out[0] = total[0]
    rows, wide = data.shape
    deep = weight.shape[0]
    width = wide // PARTS
    tail = deep - wide
    edges = [i * width for i in range(PARTS)] + [wide, deep]
    pieces = [
        pltpu.make_async_copy(
            weight_in.at[pl.ds(edges[i], edges[i + 1] - edges[i]), :],
            weight.at[pl.ds(edges[i], edges[i + 1] - edges[i]), :],
            sems.at[i],
        )
        for i in range(PARTS + 1)
    ]
    for i in (PARTS, *range(PARTS)):
        pieces[i].start()
    rest = dot(slot_part(rows, 0, 0), data[:, :width])
    for i in range(1, PARTS):
        rest = rest + dot(slot_part(rows, i, 0), data[:, i * width : (i + 1) * width])
    pieces[PARTS].wait()
    pre = dot(rest[:, :tail].astype(BF), weight[wide:, :])
    for i in range(PARTS):
        pieces[i].wait()
        pre = pre + dot(data[:, i * width : (i + 1) * width], weight[i * width : (i + 1) * width, :])
    sig = 1.0 / (1.0 + jnp.exp(-pre))
    act = (pre * sig).astype(BF)
    slope = sig * (1.0 + pre * (1.0 - sig))
    delta = (rest[:, tail:] * slope).astype(BF)
    turned = (((1,), (1,)), ((), ()))
    last = dot(delta, weight[wide:, :], turned).astype(BF)
    home = jnp.concatenate([last, act], axis=1)
    for i in range(PARTS):
        cols = slice(i * width, (i + 1) * width)
        grad = dot(delta, weight[cols, :], turned)
        out[:, cols] = (grad + dot(slot_part(rows, i, 1), home)).astype(BF)


def unpack_kernel(count, scale, route, gate, data, cotangent, mixed, token_grad, gate_grad):
    experts = data.shape[0] // ROWS
    main, tails = places(route[...], experts)
    local = route.shape[1]
    wide = data.shape[1]
    width = wide // PARTS
    turned = (((0,), (0,)), ((), ()))
    main = main.astype(BF)
    rest = None
    for i in range(PARTS):
        cols = slice(i * width, (i + 1) * width)
        token_grad[:, cols] = (dot(main, data[:, cols], turned) * scale[0]).astype(BF)
        more = dot(tails[i].astype(BF), data[:, cols], turned)
        rest = more if rest is None else rest + more
    tail = token_grad.shape[1] - wide
    token_grad[:, wide:] = (rest[:, :tail] * scale[0]).astype(BF)
    act = rest[:, tail:]
    mixed[...] = (column(gate[...]) * act).astype(BF)
    total = jnp.sum(act * cotangent[...].astype(F32), axis=1, keepdims=True)
    factor = jnp.where(iota((1, local), 1) < count[0], scale[0], 0.0)
    gate_grad[...] = line(total) * factor


VM = pl.BlockSpec(memory_space=pltpu.VMEM)
SM = pl.BlockSpec(memory_space=pltpu.SMEM)
HB = pl.BlockSpec(memory_space=pltpu.HBM)


def call(kernel, ins, outs, shapes, name, flops, scratch=(), room=32 << 20):
    return pl.pallas_call(
        kernel,
        in_specs=ins,
        out_specs=outs,
        out_shape=shapes,
        scratch_shapes=scratch,
        name=name,
        cost_estimate=pl.CostEstimate(flops=flops, bytes_accessed=10_000_000, transcendentals=0),
        compiler_params=pltpu.CompilerParams(vmem_limit_bytes=room),
    )


def shards(tokens, routes, gates, counts, expert_weight, cotangent):
    local, deep = tokens.shape
    units = cotangent.shape[1]
    experts = lax.axis_size("x") * lax.axis_size("zh") * lax.axis_size("core")
    devices = experts * lax.axis_size("y") * lax.axis_size("zl")
    group = ("x", "zh", "core")
    rows = experts * ROWS
    wide = (deep + units) * SLOTS // ROWS
    route = routes.reshape(1, local)
    gate = gates.reshape(1, local)
    weight = expert_weight[0]
    payload = call(
        pack_kernel,
        [SM, HB, HB, HB, HB],
        HB,
        jax.ShapeDtypeStruct((rows, wide), BF),
        "pack",
        2 * rows * local * 2 * wide,
        [
            pltpu.VMEM((1, local), jnp.int32),
            pltpu.VMEM((1, local), F32),
            pltpu.VMEM((local, deep), BF),
            pltpu.VMEM((local, units), BF),
            pltpu.VMEM((rows, wide), BF),
            pltpu.SemaphoreType.DMA((2 * PARTS + 4,)),
        ],
        room=67_043_328,
    )(counts, route, gate, tokens, cotangent)
    arrived = lax.all_to_all(
        payload.reshape(experts, ROWS, wide), group, split_axis=0, concat_axis=0, tiled=True
    )
    total = counts.astype(F32)
    for axis in ("y", "zl", "core"):
        total = lax.psum(total, axis)
    back, total = call(
        expert_kernel,
        [SM, VM, HB],
        [VM, SM],
        [jax.ShapeDtypeStruct((rows, wide), BF), jax.ShapeDtypeStruct((1,), F32)],
        "expert",
        4 * rows * deep * units,
        [pltpu.VMEM((deep, units), BF), pltpu.SemaphoreType.DMA((PARTS + 1,))],
        room=58 << 20,
    )(total, arrived.reshape(rows, wide), weight)
    home = lax.all_to_all(
        back.reshape(experts, ROWS, wide), group, split_axis=0, concat_axis=0, tiled=True
    )
    for axis in ("zh", "x"):
        total = lax.psum(total, axis)
    scale = jnp.float32(local * devices) / total
    mixed, token_grad, gate_grad = call(
        unpack_kernel,
        [SM, SM, VM, VM, VM, VM],
        [VM, VM, VM],
        [
            jax.ShapeDtypeStruct((local, units), BF),
            jax.ShapeDtypeStruct((local, deep), BF),
            jax.ShapeDtypeStruct((1, local), F32),
        ],
        "unpack",
        2 * rows * local * 2 * wide,
    )(counts, scale, route, gate, home.reshape(rows, wide), cotangent)
    return (mixed, token_grad, gate_grad.reshape(local, 1))


def solution(mesh):
    fine = Mesh(mesh.devices.reshape(8, 4, 8, 2, 2), ("y", "zl", "x", "zh", "core"))
    every = ("y", "zl", "x", "zh", "core")
    placed = (
        P(every, None),
        P(every, None),
        P(every, None),
        P(every),
        P(("x", "zh", "core"), None, None),
        P(every, None),
    )
    return jax.shard_map(
        shards,
        mesh=fine,
        in_specs=placed,
        out_specs=(P(every, None), P(every, None), P(every, None)),
        check_vma=False,
    )
```

```python
import functools

import jax
import jax.numpy as jnp
from jax import lax
from jax.experimental import pallas as pl
from jax.experimental.pallas import tpu as pltpu
from jax.sharding import Mesh, PartitionSpec as P

ROWS = 8
SLOTS = 6
PARTS = 3
STEP = 64.0
LANES = 128
CHUNKS = 7
FLIGHT = 3
EXPERT_ROOM = 50 << 20

BF = jnp.bfloat16
F32 = jnp.float32


def dot(a, b, dims=(((1,), (0,)), ((), ()))):
    return lax.dot_general(a, b, dims, preferred_element_type=F32)


def iota(shape, axis):
    return lax.broadcasted_iota(jnp.int32, shape, axis)


def places(route, experts):
    tokens = route.shape[1]
    choose = (iota((experts, tokens), 0) == route).astype(F32)
    before = (iota((tokens, tokens), 0) < iota((tokens, tokens), 1)).astype(BF)
    rank = jnp.sum(dot(choose.astype(BF), before) * choose, axis=0, keepdims=True).astype(jnp.int32)
    late = (rank >= PARTS).astype(jnp.int32)
    part = rank - PARTS * late
    row = iota((experts * ROWS, tokens), 0)
    main = row == route * ROWS + rank
    tail = row == route * ROWS + (SLOTS + late)
    return main, [jnp.logical_and(tail, part == i) for i in range(PARTS)]


def column(row):
    n = row.shape[1]
    return jnp.sum(jnp.where(iota((n, n), 0) == iota((n, n), 1), row, 0.0), axis=1, keepdims=True)


def line(col):
    n = col.shape[0]
    return jnp.sum(jnp.where(iota((n, n), 0) == iota((n, n), 1), col, 0.0), axis=0, keepdims=True)


def slot_part(rows, part, axis):
    slot, tail = iota((rows, rows), axis), iota((rows, rows), 1 - axis)
    inner = jnp.bitwise_and(tail, ROWS - 1)
    want = tail - inner + PARTS * (inner - SLOTS) + part
    return jnp.logical_and(inner >= SLOTS, slot == want).astype(BF)


def pack_kernel(count, route_in, gate_in, tokens_in, cotangent_in, out_hbm, route, gate, tokens, cotangent, out, sems):
    local, deep = tokens.shape
    wide = out.shape[1]
    width = wide // PARTS
    edges = [i * width for i in range(PARTS)] + [wide, deep]

    def piece(i):
        cols = pl.ds(edges[i], edges[i + 1] - edges[i])
        return pltpu.make_async_copy(tokens_in.at[:, cols], tokens.at[:, cols], sems.at[i])

    small = [
        pltpu.make_async_copy(route_in, route, sems.at[PARTS + 1]),
        pltpu.make_async_copy(gate_in, gate, sems.at[PARTS + 2]),
    ]
    side = pltpu.make_async_copy(cotangent_in, cotangent, sems.at[PARTS + 3])
    pieces = [piece(i) for i in range(PARTS + 1)]
    for copy in small + [pieces[PARTS], side] + pieces[:PARTS]:
        copy.start()
    for copy in small:
        copy.wait()
    main, tails = places(route[...], out.shape[0] // ROWS)
    weight = jnp.where(iota((1, local), 1) < count[0], gate[...], 0.0)
    main = main.astype(BF)
    factors = [
        jnp.sum(jnp.where(tail, weight, 0.0), axis=1, keepdims=True) for tail in tails
    ]
    pieces[PARTS].wait()
    side.wait()
    sent = []
    for i in range(PARTS):
        cols = slice(i * width, (i + 1) * width)
        place = tails[i].astype(BF)
        rest = jnp.concatenate(
            [dot(place, tokens[:, wide:]), dot(place, cotangent[...]) * factors[i]], axis=1
        )
        pieces[i].wait()
        out[:, cols] = (dot(main, tokens[:, cols]) + rest).astype(BF)
        copy = pltpu.make_async_copy(
            out.at[:, pl.ds(i * width, width)],
            out_hbm.at[:, pl.ds(i * width, width)],
            sems.at[PARTS + 4 + i],
        )
        copy.start()
        sent.append(copy)
    for copy in sent:
        copy.wait()


def expert_kernel(total, data, weight_in, out, weight, sems):
    rows, wide = data.shape
    deep = weight.shape[0]
    width = wide // PARTS
    tail = deep - wide
    block = deep // CHUNKS
    order = [CHUNKS - 1, *range(CHUNKS - 1)]
    pieces = [
        pltpu.make_async_copy(
            weight_in.at[pl.ds(i * block, block), :], weight.at[pl.ds(i * block, block), :], sems.at[i]
        )
        for i in order
    ]
    for piece in pieces[:FLIGHT]:
        piece.start()
    rest = dot(slot_part(rows, 0, 0), data[:, :width])
    for i in range(1, PARTS):
        rest = rest + dot(slot_part(rows, i, 0), data[:, i * width : (i + 1) * width])
    pre = None
    for k, i in enumerate(order):
        pieces[k].wait()
        if k + FLIGHT < CHUNKS:
            pieces[k + FLIGHT].start()
        left = data[:, i * block : min((i + 1) * block, wide)]
        if i == CHUNKS - 1:
            left = jnp.concatenate([left, rest[:, :tail].astype(BF)], axis=1)
        more = dot(left, weight[i * block : (i + 1) * block, :])
        pre = more if pre is None else pre + more
    sig = 1.0 / (1.0 + jnp.exp(-pre))
    act = (pre * sig).astype(BF)
    slope = sig * (1.0 + pre * (1.0 - sig))
    delta = (rest[:, tail:] * slope).astype(BF)
    turned = (((1,), (1,)), ((), ()))
    for i in order:
        start, stop = i * block, min((i + 1) * block, wide)
        grad = dot(delta, weight[start : start + block, :], turned)
        if i == CHUNKS - 1:
            home = jnp.concatenate([grad[:, stop - start :].astype(BF), act], axis=1)
            for j in range(PARTS):
                out[:, j * width : (j + 1) * width] = dot(slot_part(rows, j, 1), home).astype(BF)
        both = grad[:, : stop - start] + out[:, start:stop].astype(F32)
        out[:, start:stop] = both.astype(BF)
    high = jnp.floor(total[0] * (1.0 / STEP))
    lane = iota((rows, LANES), 1)
    note = jnp.where(lane == 0, high, jnp.where(lane == 1, total[0] - STEP * high, 0.0))
    out[:, wide:] = note.astype(BF)


def unpack_kernel(numerator, count, route, gate, data, cotangent, mixed, token_grad, gate_grad):
    rows = data.shape[0]
    experts = rows // ROWS
    main, tails = places(route[...], experts)
    local = route.shape[1]
    wide = data.shape[1] - LANES
    width = wide // PARTS
    lane = iota((rows, LANES), 1)
    first = jnp.bitwise_and(iota((rows, LANES), 0), ROWS - 1) == 0
    worth = jnp.where(lane == 0, STEP, jnp.where(lane == 1, 1.0, 0.0))
    notes = jnp.where(first, data[:, wide:].astype(F32) * worth, 0.0)
    total = jnp.sum(jnp.sum(notes, axis=0, keepdims=True), axis=1, keepdims=True)
    scale = numerator / total
    turned = (((0,), (0,)), ((), ()))
    main = main.astype(BF)
    rest = None
    for i in range(PARTS):
        cols = slice(i * width, (i + 1) * width)
        token_grad[:, cols] = (dot(main, data[:, cols], turned) * scale).astype(BF)
        more = dot(tails[i].astype(BF), data[:, cols], turned)
        rest = more if rest is None else rest + more
    tail = token_grad.shape[1] - wide
    token_grad[:, wide:] = (rest[:, :tail] * scale).astype(BF)
    act = rest[:, tail:]
    mixed[...] = (column(gate[...]) * act).astype(BF)
    dots = jnp.sum(act * cotangent[...].astype(F32), axis=1, keepdims=True)
    factor = jnp.where(iota((1, local), 1) < count[0], scale, 0.0)
    gate_grad[...] = line(dots) * factor


VM = pl.BlockSpec(memory_space=pltpu.VMEM)
SM = pl.BlockSpec(memory_space=pltpu.SMEM)
HB = pl.BlockSpec(memory_space=pltpu.HBM)


def call(kernel, ins, outs, shapes, name, flops, scratch=(), room=32 << 20):
    return pl.pallas_call(
        kernel,
        in_specs=ins,
        out_specs=outs,
        out_shape=shapes,
        scratch_shapes=scratch,
        name=name,
        cost_estimate=pl.CostEstimate(flops=flops, bytes_accessed=10_000_000, transcendentals=0),
        compiler_params=pltpu.CompilerParams(vmem_limit_bytes=room),
    )


def shards(tokens, routes, gates, counts, expert_weight, cotangent):
    local, deep = tokens.shape
    units = cotangent.shape[1]
    experts = lax.axis_size("x") * lax.axis_size("zh") * lax.axis_size("core")
    devices = experts * lax.axis_size("y") * lax.axis_size("zl")
    group = ("x", "zh", "core")
    rows = experts * ROWS
    wide = (deep + units) * SLOTS // ROWS
    route = routes.reshape(1, local)
    gate = gates.reshape(1, local)
    weight = expert_weight[0]
    payload = call(
        pack_kernel,
        [SM, HB, HB, HB, HB],
        HB,
        jax.ShapeDtypeStruct((rows, wide), BF),
        "pack",
        2 * rows * local * 2 * wide,
        [
            pltpu.VMEM((1, local), jnp.int32),
            pltpu.VMEM((1, local), F32),
            pltpu.VMEM((local, deep), BF),
            pltpu.VMEM((local, units), BF),
            pltpu.VMEM((rows, wide), BF),
            pltpu.SemaphoreType.DMA((2 * PARTS + 4,)),
        ],
        room=67_043_328,
    )(counts, route, gate, tokens, cotangent)
    arrived = lax.all_to_all(
        payload.reshape(experts, ROWS, wide), group, split_axis=0, concat_axis=0, tiled=True
    )
    total = lax.psum(counts.astype(F32), "y")
    size, apart = lax.axis_size("zl"), 1
    while apart < size:
        total = total + lax.ppermute(total, "zl", [(i, i ^ apart) for i in range(size)])
        apart = 2 * apart
    back = call(
        expert_kernel,
        [SM, VM, HB],
        VM,
        jax.ShapeDtypeStruct((rows, wide + LANES), BF),
        "expert",
        4 * rows * deep * units,
        [pltpu.VMEM((deep, units), BF), pltpu.SemaphoreType.DMA((CHUNKS,))],
        room=EXPERT_ROOM,
    )(total, arrived.reshape(rows, wide), weight)
    home = lax.all_to_all(
        back.reshape(experts, ROWS, wide + LANES), group, split_axis=0, concat_axis=0, tiled=True
    )
    mixed, token_grad, gate_grad = call(
        functools.partial(unpack_kernel, float(local * devices)),
        [SM, VM, VM, VM, VM],
        [VM, VM, VM],
        [
            jax.ShapeDtypeStruct((local, units), BF),
            jax.ShapeDtypeStruct((local, deep), BF),
            jax.ShapeDtypeStruct((1, local), F32),
        ],
        "unpack",
        2 * rows * local * 2 * wide,
    )(counts, route, gate, home.reshape(rows, wide + LANES), cotangent)
    return (mixed, token_grad, gate_grad.reshape(local, 1))


def solution(mesh):
    fine = Mesh(mesh.devices.reshape(8, 4, 8, 2, 2), ("y", "zl", "x", "zh", "core"))
    every = ("y", "zl", "x", "zh", "core")
    placed = (
        P(every, None),
        P(every, None),
        P(every, None),
        P(every),
        P(("x", "zh", "core"), None, None),
        P(every, None),
    )
    return jax.shard_map(
        shards,
        mesh=fine,
        in_specs=placed,
        out_specs=(P(every, None), P(every, None), P(every, None)),
        check_vma=False,
    )
```

```python
import jax
import jax.numpy as jnp
from jax import lax
from jax.experimental import pallas as pl
from jax.experimental.pallas import tpu as pltpu
from jax.sharding import Mesh, PartitionSpec as P

ROWS = 8
SLOTS = 6
PARTS = 3
CHUNKS = 7
FLIGHT = 3
EXPERT_ROOM = 50 << 20

BF = jnp.bfloat16
F32 = jnp.float32


def dot(a, b, dims=(((1,), (0,)), ((), ()))):
    return lax.dot_general(a, b, dims, preferred_element_type=F32)


def iota(shape, axis):
    return lax.broadcasted_iota(jnp.int32, shape, axis)


def places(route, experts):
    tokens = route.shape[1]
    choose = (iota((experts, tokens), 0) == route).astype(F32)
    before = (iota((tokens, tokens), 0) < iota((tokens, tokens), 1)).astype(BF)
    rank = jnp.sum(dot(choose.astype(BF), before) * choose, axis=0, keepdims=True).astype(jnp.int32)
    late = (rank >= PARTS).astype(jnp.int32)
    part = rank - PARTS * late
    row = iota((experts * ROWS, tokens), 0)
    main = row == route * ROWS + rank
    tail = row == route * ROWS + (SLOTS + late)
    return main, [jnp.logical_and(tail, part == i) for i in range(PARTS)]


def column(row):
    n = row.shape[1]
    return jnp.sum(jnp.where(iota((n, n), 0) == iota((n, n), 1), row, 0.0), axis=1, keepdims=True)


def line(col):
    n = col.shape[0]
    return jnp.sum(jnp.where(iota((n, n), 0) == iota((n, n), 1), col, 0.0), axis=0, keepdims=True)


def slot_part(rows, part, axis):
    slot, tail = iota((rows, rows), axis), iota((rows, rows), 1 - axis)
    inner = jnp.bitwise_and(tail, ROWS - 1)
    want = tail - inner + PARTS * (inner - SLOTS) + part
    return jnp.logical_and(inner >= SLOTS, slot == want).astype(BF)


def pack_kernel(count, route_in, gate_in, tokens_in, cotangent_in, out_hbm, route, gate, tokens, cotangent, out, sems):
    local, deep = tokens.shape
    wide = out.shape[1]
    width = wide // PARTS
    edges = [i * width for i in range(PARTS)] + [wide, deep]

    def piece(i):
        cols = pl.ds(edges[i], edges[i + 1] - edges[i])
        return pltpu.make_async_copy(tokens_in.at[:, cols], tokens.at[:, cols], sems.at[i])

    small = [
        pltpu.make_async_copy(route_in, route, sems.at[PARTS + 1]),
        pltpu.make_async_copy(gate_in, gate, sems.at[PARTS + 2]),
    ]
    side = pltpu.make_async_copy(cotangent_in, cotangent, sems.at[PARTS + 3])
    pieces = [piece(i) for i in range(PARTS + 1)]
    for copy in small + [pieces[PARTS], side] + pieces[:PARTS]:
        copy.start()
    for copy in small:
        copy.wait()
    main, tails = places(route[...], out.shape[0] // ROWS)
    weight = jnp.where(iota((1, local), 1) < count[0], gate[...], 0.0)
    main = main.astype(BF)
    factors = [
        jnp.sum(jnp.where(tail, weight, 0.0), axis=1, keepdims=True) for tail in tails
    ]
    pieces[PARTS].wait()
    side.wait()
    sent = []
    for i in range(PARTS):
        cols = slice(i * width, (i + 1) * width)
        place = tails[i].astype(BF)
        rest = jnp.concatenate(
            [dot(place, tokens[:, wide:]), dot(place, cotangent[...]) * factors[i]], axis=1
        )
        pieces[i].wait()
        out[:, cols] = (dot(main, tokens[:, cols]) + rest).astype(BF)
        copy = pltpu.make_async_copy(
            out.at[:, pl.ds(i * width, width)],
            out_hbm.at[:, pl.ds(i * width, width)],
            sems.at[PARTS + 4 + i],
        )
        copy.start()
        sent.append(copy)
    for copy in sent:
        copy.wait()


def expert_kernel(total, data, weight_in, out, total_out, weight, sems):
    total_out[0] = total[0]
    rows, wide = data.shape
    deep = weight.shape[0]
    width = wide // PARTS
    tail = deep - wide
    block = deep // CHUNKS
    order = [CHUNKS - 1, *range(CHUNKS - 1)]
    pieces = [
        pltpu.make_async_copy(
            weight_in.at[pl.ds(i * block, block), :], weight.at[pl.ds(i * block, block), :], sems.at[i]
        )
        for i in order
    ]
    for piece in pieces[:FLIGHT]:
        piece.start()
    rest = dot(slot_part(rows, 0, 0), data[:, :width])
    for i in range(1, PARTS):
        rest = rest + dot(slot_part(rows, i, 0), data[:, i * width : (i + 1) * width])
    pre = None
    for k, i in enumerate(order):
        pieces[k].wait()
        if k + FLIGHT < CHUNKS:
            pieces[k + FLIGHT].start()
        left = data[:, i * block : min((i + 1) * block, wide)]
        if i == CHUNKS - 1:
            left = jnp.concatenate([left, rest[:, :tail].astype(BF)], axis=1)
        more = dot(left, weight[i * block : (i + 1) * block, :])
        pre = more if pre is None else pre + more
    sig = 1.0 / (1.0 + jnp.exp(-pre))
    act = (pre * sig).astype(BF)
    slope = sig * (1.0 + pre * (1.0 - sig))
    delta = (rest[:, tail:] * slope).astype(BF)
    turned = (((1,), (1,)), ((), ()))
    for i in order:
        start, stop = i * block, min((i + 1) * block, wide)
        grad = dot(delta, weight[start : start + block, :], turned)
        if i == CHUNKS - 1:
            home = jnp.concatenate([grad[:, stop - start :].astype(BF), act], axis=1)
            for j in range(PARTS):
                out[:, j * width : (j + 1) * width] = dot(slot_part(rows, j, 1), home).astype(BF)
        both = grad[:, : stop - start] + out[:, start:stop].astype(F32)
        out[:, start:stop] = both.astype(BF)


def unpack_kernel(count, scale_in, route, gate, data, cotangent, mixed, token_grad, gate_grad):
    rows = data.shape[0]
    experts = rows // ROWS
    main, tails = places(route[...], experts)
    local = route.shape[1]
    wide = data.shape[1]
    width = wide // PARTS
    scale = scale_in[0]
    turned = (((0,), (0,)), ((), ()))
    main = main.astype(BF)
    rest = None
    for i in range(PARTS):
        cols = slice(i * width, (i + 1) * width)
        token_grad[:, cols] = (dot(main, data[:, cols], turned) * scale).astype(BF)
        more = dot(tails[i].astype(BF), data[:, cols], turned)
        rest = more if rest is None else rest + more
    tail = token_grad.shape[1] - wide
    token_grad[:, wide:] = (rest[:, :tail] * scale).astype(BF)
    act = rest[:, tail:]
    mixed[...] = (column(gate[...]) * act).astype(BF)
    dots = jnp.sum(act * cotangent[...].astype(F32), axis=1, keepdims=True)
    factor = jnp.where(iota((1, local), 1) < count[0], scale, 0.0)
    gate_grad[...] = line(dots) * factor


VM = pl.BlockSpec(memory_space=pltpu.VMEM)
SM = pl.BlockSpec(memory_space=pltpu.SMEM)
HB = pl.BlockSpec(memory_space=pltpu.HBM)


def call(kernel, ins, outs, shapes, name, flops, scratch=(), room=32 << 20):
    return pl.pallas_call(
        kernel,
        in_specs=ins,
        out_specs=outs,
        out_shape=shapes,
        scratch_shapes=scratch,
        name=name,
        cost_estimate=pl.CostEstimate(flops=flops, bytes_accessed=10_000_000, transcendentals=0),
        compiler_params=pltpu.CompilerParams(vmem_limit_bytes=room),
    )


def both(value, axis):
    size, apart = lax.axis_size(axis), 1
    while apart < size:
        value = value + lax.ppermute(value, axis, [(i, i ^ apart) for i in range(size)])
        apart = 2 * apart
    return value


def shards(tokens, routes, gates, counts, expert_weight, cotangent):
    local, deep = tokens.shape
    units = cotangent.shape[1]
    experts = lax.axis_size("x") * lax.axis_size("zh") * lax.axis_size("core")
    devices = experts * lax.axis_size("y") * lax.axis_size("zl")
    group = ("x", "zh", "core")
    rows = experts * ROWS
    wide = (deep + units) * SLOTS // ROWS
    route = routes.reshape(1, local)
    gate = gates.reshape(1, local)
    weight = expert_weight[0]
    payload = call(
        pack_kernel,
        [SM, HB, HB, HB, HB],
        HB,
        jax.ShapeDtypeStruct((rows, wide), BF),
        "pack",
        2 * rows * local * 2 * wide,
        [
            pltpu.VMEM((1, local), jnp.int32),
            pltpu.VMEM((1, local), F32),
            pltpu.VMEM((local, deep), BF),
            pltpu.VMEM((local, units), BF),
            pltpu.VMEM((rows, wide), BF),
            pltpu.SemaphoreType.DMA((2 * PARTS + 4,)),
        ],
        room=67_043_328,
    )(counts, route, gate, tokens, cotangent)
    arrived = lax.all_to_all(
        payload.reshape(experts, ROWS, wide), group, split_axis=0, concat_axis=0, tiled=True
    )
    total = both(both(lax.psum(counts.astype(F32), "y"), "zl"), "core")
    back, total = call(
        expert_kernel,
        [SM, VM, HB],
        [VM, SM],
        [jax.ShapeDtypeStruct((rows, wide), BF), jax.ShapeDtypeStruct((1,), F32)],
        "expert",
        4 * rows * deep * units,
        [pltpu.VMEM((deep, units), BF), pltpu.SemaphoreType.DMA((CHUNKS,))],
        room=EXPERT_ROOM,
    )(total, arrived.reshape(rows, wide), weight)
    home = lax.all_to_all(
        back.reshape(experts, ROWS, wide), group, split_axis=0, concat_axis=0, tiled=True
    )
    total = both(both(total, "zh"), "x")
    scale = jnp.float32(local * devices) / total
    mixed, token_grad, gate_grad = call(
        unpack_kernel,
        [SM, SM, VM, VM, VM, VM],
        [VM, VM, VM],
        [
            jax.ShapeDtypeStruct((local, units), BF),
            jax.ShapeDtypeStruct((local, deep), BF),
            jax.ShapeDtypeStruct((1, local), F32),
        ],
        "unpack",
        2 * rows * local * 2 * wide,
    )(counts, scale, route, gate, home.reshape(rows, wide), cotangent)
    return (mixed, token_grad, gate_grad.reshape(local, 1))


def solution(mesh):
    fine = Mesh(mesh.devices.reshape(8, 4, 8, 2, 2), ("y", "zl", "x", "zh", "core"))
    every = ("y", "zl", "x", "zh", "core")
    placed = (
        P(every, None),
        P(every, None),
        P(every, None),
        P(every),
        P(("x", "zh", "core"), None, None),
        P(every, None),
    )
    return jax.shard_map(
        shards,
        mesh=fine,
        in_specs=placed,
        out_specs=(P(every, None), P(every, None), P(every, None)),
        check_vma=False,
    )
```

```python
import functools

import jax
import jax.numpy as jnp
from jax import lax
from jax.experimental import pallas as pl
from jax.experimental.pallas import tpu as pltpu
from jax.sharding import Mesh, PartitionSpec as P

ROWS = 8
SLOTS = 6
PARTS = 3
STEP = 64.0
LANES = 128
CHUNKS = 7
FLIGHT = 3
EXPERT_ROOM = 50 << 20

BF = jnp.bfloat16
F32 = jnp.float32


def dot(a, b, dims=(((1,), (0,)), ((), ()))):
    return lax.dot_general(a, b, dims, preferred_element_type=F32)


def iota(shape, axis):
    return lax.broadcasted_iota(jnp.int32, shape, axis)


def turned_order(index, experts):
    return jnp.bitwise_and(3 * jnp.right_shift(index, 2), experts // 4 - 1) * 4 + jnp.bitwise_and(index, 3)


def places(route, experts):
    route = turned_order(route, experts)
    tokens = route.shape[1]
    choose = (iota((experts, tokens), 0) == route).astype(F32)
    before = (iota((tokens, tokens), 0) < iota((tokens, tokens), 1)).astype(BF)
    rank = jnp.sum(dot(choose.astype(BF), before) * choose, axis=0, keepdims=True).astype(jnp.int32)
    late = (rank >= PARTS).astype(jnp.int32)
    part = rank - PARTS * late
    row = iota((experts * ROWS, tokens), 0)
    main = row == route * ROWS + rank
    tail = row == route * ROWS + (SLOTS + late)
    return main, [jnp.logical_and(tail, part == i) for i in range(PARTS)]


def column(row):
    n = row.shape[1]
    return jnp.sum(jnp.where(iota((n, n), 0) == iota((n, n), 1), row, 0.0), axis=1, keepdims=True)


def line(col):
    n = col.shape[0]
    return jnp.sum(jnp.where(iota((n, n), 0) == iota((n, n), 1), col, 0.0), axis=0, keepdims=True)


def slot_part(rows, part, axis):
    slot, tail = iota((rows, rows), axis), iota((rows, rows), 1 - axis)
    inner = jnp.bitwise_and(tail, ROWS - 1)
    want = tail - inner + PARTS * (inner - SLOTS) + part
    return jnp.logical_and(inner >= SLOTS, slot == want).astype(BF)


def pack_kernel(count, route_in, gate_in, tokens_in, cotangent_in, out_hbm, route, gate, tokens, cotangent, out, sems):
    local, deep = tokens.shape
    wide = out.shape[1]
    width = wide // PARTS
    edges = [i * width for i in range(PARTS)] + [wide, deep]

    def piece(i):
        cols = pl.ds(edges[i], edges[i + 1] - edges[i])
        return pltpu.make_async_copy(tokens_in.at[:, cols], tokens.at[:, cols], sems.at[i])

    small = [
        pltpu.make_async_copy(route_in, route, sems.at[PARTS + 1]),
        pltpu.make_async_copy(gate_in, gate, sems.at[PARTS + 2]),
    ]
    side = pltpu.make_async_copy(cotangent_in, cotangent, sems.at[PARTS + 3])
    pieces = [piece(i) for i in range(PARTS + 1)]
    for copy in small + [pieces[PARTS], side] + pieces[:PARTS]:
        copy.start()
    for copy in small:
        copy.wait()
    main, tails = places(route[...], out.shape[0] // ROWS)
    weight = jnp.where(iota((1, local), 1) < count[0], gate[...], 0.0)
    main = main.astype(BF)
    factors = [
        jnp.sum(jnp.where(tail, weight, 0.0), axis=1, keepdims=True) for tail in tails
    ]
    pieces[PARTS].wait()
    side.wait()
    sent = []
    for i in range(PARTS):
        cols = slice(i * width, (i + 1) * width)
        place = tails[i].astype(BF)
        rest = jnp.concatenate(
            [dot(place, tokens[:, wide:]), dot(place, cotangent[...]) * factors[i]], axis=1
        )
        pieces[i].wait()
        out[:, cols] = (dot(main, tokens[:, cols]) + rest).astype(BF)
        copy = pltpu.make_async_copy(
            out.at[:, pl.ds(i * width, width)],
            out_hbm.at[:, pl.ds(i * width, width)],
            sems.at[PARTS + 4 + i],
        )
        copy.start()
        sent.append(copy)
    for copy in sent:
        copy.wait()


def expert_kernel(total, data, weight_in, out, weight, sems):
    rows, wide = data.shape
    deep = weight.shape[0]
    width = wide // PARTS
    tail = deep - wide
    block = deep // CHUNKS
    order = [CHUNKS - 1, *range(CHUNKS - 1)]
    pieces = [
        pltpu.make_async_copy(
            weight_in.at[pl.ds(i * block, block), :], weight.at[pl.ds(i * block, block), :], sems.at[i]
        )
        for i in order
    ]
    for piece in pieces[:FLIGHT]:
        piece.start()
    rest = dot(slot_part(rows, 0, 0), data[:, :width])
    for i in range(1, PARTS):
        rest = rest + dot(slot_part(rows, i, 0), data[:, i * width : (i + 1) * width])
    pre = None
    for k, i in enumerate(order):
        pieces[k].wait()
        if k + FLIGHT < CHUNKS:
            pieces[k + FLIGHT].start()
        left = data[:, i * block : min((i + 1) * block, wide)]
        if i == CHUNKS - 1:
            left = jnp.concatenate([left, rest[:, :tail].astype(BF)], axis=1)
        more = dot(left, weight[i * block : (i + 1) * block, :])
        pre = more if pre is None else pre + more
    sig = 1.0 / (1.0 + jnp.exp(-pre))
    act = (pre * sig).astype(BF)
    slope = sig * (1.0 + pre * (1.0 - sig))
    delta = (rest[:, tail:] * slope).astype(BF)
    turned = (((1,), (1,)), ((), ()))
    for i in order:
        start, stop = i * block, min((i + 1) * block, wide)
        grad = dot(delta, weight[start : start + block, :], turned)
        if i == CHUNKS - 1:
            home = jnp.concatenate([grad[:, stop - start :].astype(BF), act], axis=1)
            for j in range(PARTS):
                out[:, j * width : (j + 1) * width] = dot(slot_part(rows, j, 1), home).astype(BF)
        both = grad[:, : stop - start] + out[:, start:stop].astype(F32)
        out[:, start:stop] = both.astype(BF)
    high = jnp.floor(total[0] * (1.0 / STEP))
    lane = iota((rows, LANES), 1)
    note = jnp.where(lane == 0, high, jnp.where(lane == 1, total[0] - STEP * high, 0.0))
    out[:, wide:] = note.astype(BF)


def unpack_kernel(numerator, count, route, gate, data, cotangent, mixed, token_grad, gate_grad):
    rows = data.shape[0]
    experts = rows // ROWS
    main, tails = places(route[...], experts)
    local = route.shape[1]
    wide = data.shape[1] - LANES
    width = wide // PARTS
    lane = iota((rows, LANES), 1)
    first = jnp.bitwise_and(iota((rows, LANES), 0), ROWS - 1) == 0
    worth = jnp.where(lane == 0, STEP, jnp.where(lane == 1, 1.0, 0.0))
    notes = jnp.where(first, data[:, wide:].astype(F32) * worth, 0.0)
    total = jnp.sum(jnp.sum(notes, axis=0, keepdims=True), axis=1, keepdims=True)
    scale = numerator / total
    turned = (((0,), (0,)), ((), ()))
    main = main.astype(BF)
    rest = None
    for i in range(PARTS):
        cols = slice(i * width, (i + 1) * width)
        token_grad[:, cols] = (dot(main, data[:, cols], turned) * scale).astype(BF)
        more = dot(tails[i].astype(BF), data[:, cols], turned)
        rest = more if rest is None else rest + more
    tail = token_grad.shape[1] - wide
    token_grad[:, wide:] = (rest[:, :tail] * scale).astype(BF)
    act = rest[:, tail:]
    mixed[...] = (column(gate[...]) * act).astype(BF)
    dots = jnp.sum(act * cotangent[...].astype(F32), axis=1, keepdims=True)
    factor = jnp.where(iota((1, local), 1) < count[0], scale, 0.0)
    gate_grad[...] = line(dots) * factor


VM = pl.BlockSpec(memory_space=pltpu.VMEM)
SM = pl.BlockSpec(memory_space=pltpu.SMEM)
HB = pl.BlockSpec(memory_space=pltpu.HBM)


def call(kernel, ins, outs, shapes, name, flops, scratch=(), room=32 << 20):
    return pl.pallas_call(
        kernel,
        in_specs=ins,
        out_specs=outs,
        out_shape=shapes,
        scratch_shapes=scratch,
        name=name,
        cost_estimate=pl.CostEstimate(flops=flops, bytes_accessed=10_000_000, transcendentals=0),
        compiler_params=pltpu.CompilerParams(vmem_limit_bytes=room),
    )


def shards(tokens, routes, gates, counts, expert_weight, cotangent):
    local, deep = tokens.shape
    units = cotangent.shape[1]
    experts = lax.axis_size("x") * lax.axis_size("zh") * lax.axis_size("core")
    devices = experts * lax.axis_size("y") * lax.axis_size("zl")
    group = ("x", "zh", "core")
    order = [[(3 * (i // 4)) % (experts // 4) * 4 + i % 4 for i in range(experts)]]
    rows = experts * ROWS
    wide = (deep + units) * SLOTS // ROWS
    route = routes.reshape(1, local)
    gate = gates.reshape(1, local)
    weight = expert_weight[0]
    payload = call(
        pack_kernel,
        [SM, HB, HB, HB, HB],
        HB,
        jax.ShapeDtypeStruct((rows, wide), BF),
        "pack",
        2 * rows * local * 2 * wide,
        [
            pltpu.VMEM((1, local), jnp.int32),
            pltpu.VMEM((1, local), F32),
            pltpu.VMEM((local, deep), BF),
            pltpu.VMEM((local, units), BF),
            pltpu.VMEM((rows, wide), BF),
            pltpu.SemaphoreType.DMA((2 * PARTS + 4,)),
        ],
        room=67_043_328,
    )(counts, route, gate, tokens, cotangent)
    arrived = lax.all_to_all(
        payload.reshape(experts, ROWS, wide), group, split_axis=0, concat_axis=0, tiled=True,
        axis_index_groups=order
    )
    total = lax.psum(counts.astype(F32), "y")
    size, apart = lax.axis_size("zl"), 1
    while apart < size:
        total = total + lax.ppermute(total, "zl", [(i, i ^ apart) for i in range(size)])
        apart = 2 * apart
    back = call(
        expert_kernel,
        [SM, VM, HB],
        VM,
        jax.ShapeDtypeStruct((rows, wide + LANES), BF),
        "expert",
        4 * rows * deep * units,
        [pltpu.VMEM((deep, units), BF), pltpu.SemaphoreType.DMA((CHUNKS,))],
        room=EXPERT_ROOM,
    )(total, arrived.reshape(rows, wide), weight)
    home = lax.all_to_all(
        back.reshape(experts, ROWS, wide + LANES), group, split_axis=0, concat_axis=0, tiled=True,
        axis_index_groups=order
    )
    mixed, token_grad, gate_grad = call(
        functools.partial(unpack_kernel, float(local * devices)),
        [SM, VM, VM, VM, VM],
        [VM, VM, VM],
        [
            jax.ShapeDtypeStruct((local, units), BF),
            jax.ShapeDtypeStruct((local, deep), BF),
            jax.ShapeDtypeStruct((1, local), F32),
        ],
        "unpack",
        2 * rows * local * 2 * wide,
    )(counts, route, gate, home.reshape(rows, wide + LANES), cotangent)
    return (mixed, token_grad, gate_grad.reshape(local, 1))


def solution(mesh):
    fine = Mesh(mesh.devices.reshape(8, 4, 8, 2, 2), ("y", "zl", "x", "zh", "core"))
    every = ("y", "zl", "x", "zh", "core")
    placed = (
        P(every, None),
        P(every, None),
        P(every, None),
        P(every),
        P(("x", "zh", "core"), None, None),
        P(every, None),
    )
    return jax.shard_map(
        shards,
        mesh=fine,
        in_specs=placed,
        out_specs=(P(every, None), P(every, None), P(every, None)),
        check_vma=False,
    )
```
